128 devices in a mesh: row: 8 (over y, core), col: 16 (over z, x).
Axes of the slice: x: 4, y: 4, z: 4, core: 2. Of those that a mesh axis runs over, the one named last changes fastest.
Arguments:
- panel: bfloat16 [256, 512, 128], P('row', 'col'), may hold values from -1.296875 to 1.296875
- bases: bfloat16 [256, 1024, 128], P('row', 'col'), may hold values from -0.5 to 0.5
- pivots: float32 [512], P('col'), may hold values from 0.25 to 4
- ranks: int32 [256], P('row'), may hold values from 32 to 128
- pairs: int32 [256, 2], P('row'), may hold values from 0 to 255, as said below
- targets: bfloat16 [256, 1024, 1024], P('row', 'col'), may hold values from -6 to 6
Outputs:
- updated: bfloat16 [256, 1024, 1024], P('row', 'col')
The draws below stay inside these ranges and needn't reach their ends.
Inputs may be any that keep to these rules, and one draw needn't show every extreme that they name: Row p has column tile j = pairs[p, 1] in [b * 32, (b + 1) * 32) with b = p // 32, and row tile i = pairs[p, 0] with j <= i.
All inputs are finite; a program needn't handle non-finite values.
Results may differ from the reference program's by a relative error of at most 0.0056.
Values may be sent and summed in bfloat16 or wider, within the bound.
A program may use at most 128 MiB of HBM per device.

```python
import math
import jax
import jax.numpy as jnp
from jax import lax

B = 1024
R = 128
W = 512
TPR = 32
P_ROW = 32
NT = 256
NPAIRS = 256


def draw_pairs(key, part):
    base = jax.random.fold_in(key, 7)
    first_key, second_key = jax.random.split(base)
    blocks = jnp.arange(NPAIRS, dtype=jnp.int32) // P_ROW
    col_tile = blocks * TPR + jax.random.randint(first_key, (NPAIRS,), 0, TPR, dtype=jnp.int32)
    spread = (NT - col_tile).astype(jnp.int32)
    row_tile = col_tile + jax.random.randint(second_key, (NPAIRS,), 0, spread, dtype=jnp.int32)
    return jnp.stack([row_tile, col_tile], axis=1).astype(jnp.int32)


def plant(array, own_key, least, high):
    longest = array.shape.index(max(array.shape))
    spots = []
    for shift in (0, 1):
        where = [jax.random.randint(jax.random.fold_in(own_key, axis), (), 0, length) for axis, length in enumerate(array.shape)]
        where[longest] = (where[longest] + shift) % array.shape[longest]
        spots.append(tuple(where))
    return array.at[spots[0]].set(least).at[spots[1]].set(high)


def block_levels(rng, dims, cuts, least, largest):
    def one(position, blocks):
        draws = jax.random.uniform(jax.random.fold_in(jax.random.fold_in(rng, 6), position), (blocks,), jnp.float32, least / len(cuts), largest / len(cuts))
        return jnp.repeat(jnp.exp(draws), dims[position] // blocks).reshape((-1,) + (1,) * (len(dims) - position - 1))

    loudness = one(*cuts[0])
    for cut in cuts[1:]:
        loudness = loudness * one(*cut)
    return loudness


def noise(rng, extent, scale, bound, cuts=(), held_as=jnp.bfloat16):
    level = block_levels(rng, extent, cuts, -0.22, 0.18) if cuts else 1.0
    array = jax.random.normal(rng, extent, jnp.float32) * scale * level
    return jnp.minimum(jnp.maximum(array, -bound), bound).astype(held_as)


def setup_inputs(seed: int = 0) -> dict:
    splits = jax.random.split(jax.random.key(seed), 7)
    return {
        "panel": noise(splits[0], (NT, W, R), 0.21, 1.296875, ((0, 8), (1, 16))),
        "bases": noise(splits[1], (NT, B, R), R ** -0.5, 0.5, ((0, 8), (1, 16))),
        "pivots": jnp.clip(jnp.exp(math.log(4.0) - 2.7725887 * jax.random.uniform(splits[2], (W,), jnp.float32) ** block_levels(splits[2], (W,), ((0, 16),), -0.2, 0.2)), 0.25, 4.0),
        "ranks": plant(jax.random.randint(splits[3], (NT,), R // 4, R + 1), jax.random.fold_in(splits[3], 1), R // 4, R).astype(jnp.int32),
        "pairs": draw_pairs(jax.random.fold_in(splits[6], 71), 0),
        "targets": noise(splits[5], (NPAIRS, B, B), 1.0, 6.0, ((0, 8), (1, 16))),
    }


def reference(panel, bases, pivots, ranks, pairs, targets):
    keep = lax.broadcasted_iota(jnp.int32, (1, 1, panel.shape[2]), 2) < ranks[:, None, None]
    masked = jnp.where(keep, panel, jnp.zeros_like(panel))
    scaled = (masked.astype(jnp.float32) * pivots[None, :, None]).astype(jnp.bfloat16)

    def one_pair(item):
        pair, target = item
        row_tile = pair[0]
        col_tile = pair[1]
        core = jnp.dot(scaled[row_tile].T, masked[col_tile], preferred_element_type=jnp.float32)
        core_b = core.astype(jnp.bfloat16)
        factor = jnp.dot(core_b, bases[col_tile].T, preferred_element_type=jnp.float32).astype(jnp.bfloat16)
        update = jnp.dot(bases[row_tile], factor, preferred_element_type=jnp.float32)
        return (target.astype(jnp.float32) - update).astype(jnp.bfloat16)

    return lax.map(one_pair, (pairs, targets))
```

```python
import jax
import jax.numpy as jnp
from jax import lax
from jax.experimental import pallas as pl
from jax.experimental.pallas import tpu as pltpu
from jax.sharding import PartitionSpec as P

MESH = pl.DeviceIdType.MESH
F32 = jnp.float32
BF16 = jnp.bfloat16
SIDE = 4


def wrap(v):
    return lax.rem(v + 2 * SIDE, SIDE)


def near(d):
    return (d + 1) % SIDE - 1


def kernel(
    panel, bases, pivots, ranks, pairs, targets, out,
    here, above, below, across, lefts, tiles, mine, ready, transit, operands, cores, lead, held, scale,
    send_sem, recv_sem, local_sem,
):
    row = lax.axis_index("row")
    col = lax.axis_index("col")
    y, core = lax.div(row, 2), lax.rem(row, 2)
    z, x = lax.div(col, SIDE), lax.rem(col, SIDE)
    n_tiles, depth, rank = panel.shape
    part = bases.shape[1]
    half = n_tiles // 2
    n_pairs = held.shape[0]
    whole = {0: here, 1: above, -1: below, 2: across}

    def at_col(dz, dx):
        return (row, wrap(z + dz) * SIDE + wrap(x + dx))

    def at_row(dy):
        return (wrap(y + dy) * 2 + core, col)

    twin = (y * 2 + 1 - core, col)

    kept = []

    def move(src, dst):
        copy = pltpu.make_async_copy(src, dst, local_sem.at[len(kept)])
        copy.start()
        kept.append(copy)
        return copy

    own_tiles = pl.ds(row * n_tiles, n_tiles)
    get_panel = move(panel, mine)
    get_here = move(bases, here.at[x])
    get_left = move(bases, lefts.at[own_tiles])
    get_targets = move(targets, held)

    barrier = pltpu.get_barrier_semaphore()
    friends = [at_col(0, 1), at_col(0, -1), at_col(1, 0), at_col(-1, 0), at_row(1), at_row(-1), twin]
    friends += [at_col(0, 2), at_col(2, 0)]
    for friend in friends:
        pl.semaphore_signal(barrier, inc=1, device_id=friend, device_id_type=MESH)
    for r in range(depth):
        scale[pl.ds(r, 1), :] = jnp.full((1, rank), pivots[r], F32)
    pl.semaphore_wait(barrier, len(friends))

    sent = []

    def send(src, dst, to):
        k = len(sent)
        copy = pltpu.make_async_remote_copy(
            src_ref=src,
            dst_ref=dst,
            send_sem=send_sem.at[k],
            recv_sem=recv_sem.at[k],
            device_id=to,
            device_id_type=MESH,
        )
        copy.start()
        sent.append(copy)
        return copy

    def pass_on(dz, at_x, to, first, count, fresh=False):
        some = pl.ds(first, count)
        src = bases.at[some] if fresh else whole[near(dz)].at[at_x, some]
        return send(src, whole[near(dz - to[0])].at[at_x, some], at_col(*to))

    def along_x(dz, first, fresh=False):
        return [pass_on(dz, x, (0, d), first, half, fresh) for d in (1, -1)]

    def along_x_far(dz, first, arriving):
        quarter = half // 2
        arriving[0].wait_recv()
        a = pass_on(dz, wrap(x - 1), (0, 1), first, quarter)
        arriving[1].wait_recv()
        b = pass_on(dz, wrap(x + 1), (0, -1), first + quarter, quarter)
        return [a, b]

    def along_z(dx, first, fresh=False):
        return [pass_on(0, wrap(x + dx), (d, 0), first, half, fresh) for d in (1, -1)]

    def along_z_far(dx, first, arriving):
        quarter = half // 2
        arriving[0].wait_recv()
        a = pass_on(-1, wrap(x + dx), (1, 0), first, quarter)
        arriving[1].wait_recv()
        b = pass_on(1, wrap(x + dx), (-1, 0), first + quarter, quarter)
        return [a, b]

    def own_row(array):
        block = array.at[own_tiles]
        return [send(block, block, to) for to in (at_row(1), at_row(-1), twin)]

    def far_row(array, arriving):
        got = []
        for k, d in ((0, -1), (1, 1)):
            first = (wrap(y + d) * 2 + core) * n_tiles
            arriving[k].wait_recv()
            block = array.at[pl.ds(first + k * half, half)]
            got.append(send(block, block, at_row(-d)))
            block = array.at[pl.ds(first, n_tiles)]
            got.append(send(block, block, twin))
        return got

    def last_row(array, arriving):
        first = (wrap(y + 2) * 2 + core) * n_tiles
        got = []
        for k in (0, 1):
            arriving[2 * k].wait_recv()
            block = array.at[pl.ds(first + k * half, half)]
            got.append(send(block, block, twin))
        return got

    def wait_all(copies):
        for copy in copies:
            copy.wait_recv()

    far_x, far_z, first_z, first_x = {}, {}, {}, {}
    in_x = along_x(0, 0, True)
    in_z = along_z(0, half, True)
    first_z[0] = along_z(0, 0, True)
    first_x[0] = along_x(0, half, True)

    get_panel.wait()
    lanes = lax.broadcasted_iota(jnp.int32, (depth, rank), 1)

    @pl.loop(0, n_tiles)
    def _(t):
        tile = mine[t].astype(F32)
        tiles[row * n_tiles + t] = jnp.where(lanes < ranks[t], tile, jnp.zeros_like(tile)).astype(BF16)

    panel_in = own_row(tiles)
    panel_far = far_row(tiles, panel_in)
    get_left.wait()
    left_in = own_row(lefts)
    panel_last = last_row(tiles, panel_far)
    wait_all([panel_in[2], panel_far[1], panel_far[3], *panel_last])

    @pl.loop(0, n_pairs)
    def _(p):
        to = lax.div(p, 2)
        pr, tz, tx = lax.rem(p, 2), lax.div(to, SIDE), lax.rem(to, SIDE)
        scaled = (tiles[pairs[p, 0]].astype(F32) * scale[...]).astype(BF16)
        ready[tx, tz, 0, pr] = scaled
        ready[tx, tz, 1, pr] = tiles[pairs[p, 1]]

    own_transit = move(ready.at[x], transit.at[:, :, :, x])
    stage_x = [
        send(ready.at[wrap(x + d)], transit.at[:, :, :, x], at_col(0, d)) for d in (1, -1, 2)
    ]

    far_x[0] = along_x_far(0, 0, in_x)
    far_z[0] = along_z_far(0, half, in_z)
    for d in (-1, 1):
        first_z[d] = along_z(d, 0)
        first_x[d] = along_x(d, half)
    left_far = far_row(lefts, left_in)

    own_transit.wait()
    wait_all(stage_x)
    mid = pl.ds(z * SIDE, SIDE)
    own_operands = move(transit.at[z], operands.at[:, :, mid])
    stage_z = [
        send(transit.at[wrap(z + d)], operands.at[:, :, mid], at_col(d, 0)) for d in (1, -1, 2)
    ]

    late_z = {0: along_z_far(0, 0, first_z[0])}
    late_x = {0: along_x_far(0, half, first_x[0])}
    wait_all(far_x[0] + far_z[0])
    first_z[2] = along_z(2, 0)
    first_x[2] = along_x(2, half)
    left_last = last_row(lefts, left_far)

    own_operands.wait()
    wait_all(stage_z)
    for pr in (0, 1):
        a = operands[0, pr].reshape(SIDE * SIDE * depth, rank)
        b = operands[1, pr].reshape(SIDE * SIDE * depth, rank)
        total = lax.dot_general(a, b, (((0,), (0,)), ((), ())), preferred_element_type=F32)
        cores[z, x, pr] = total.astype(BF16)
    mine_0, mine_1 = cores.at[z, x, 0], cores.at[z, x, 1]
    core_x = [send(mine_0, mine_0, at_col(0, d)) for d in (1, -1, 2)]
    core_z = [send(mine_1, mine_1, at_col(d, 0)) for d in (1, -1, 2)]

    for d in (-1, 1):
        late_z[d] = along_z_far(d, 0, first_z[d])
        late_x[d] = along_x_far(d, half, first_x[d])

    wait_all(core_x)
    line = cores.at[z, :, 0]
    core_last = [send(line, line, at_col(d, 0)) for d in (1, -1, 2)]
    wait_all(core_z)
    line = cores.at[:, x, 1]
    core_last += [send(line, line, at_col(0, d)) for d in (1, -1, 2)]

    late_z[2] = along_z_far(2, 0, first_z[2])
    late_x[2] = along_x_far(2, half, first_x[2])

    wait_all([left_in[2], left_far[1], left_far[3], *left_last, *core_last])

    @pl.loop(0, n_pairs)
    def _(p):
        to = lax.div(p, 2)
        pr, tz, tx = lax.rem(p, 2), lax.div(to, SIDE), lax.rem(to, SIDE)
        product = jnp.dot(lefts[pairs[p, 0]], cores[tz, tx, pr], preferred_element_type=F32)
        lead[p] = product.astype(BF16)

    width = SIDE * part
    get_here.wait()
    get_targets.wait()
    done = []

    def update(dz):
        group = whole[dz]
        columns = pl.ds(pl.multiple_of(wrap(z + dz) * width, width), width)

        @pl.loop(0, n_pairs)
        def _(p):
            right = group[:, lax.rem(pairs[p, 1], n_tiles)].reshape(width, rank)
            change = lax.dot_general(
                lead[p], right, (((1,), (1,)), ((), ())), preferred_element_type=F32
            )
            held[p, :, columns] = (held[p, :, columns].astype(F32) - change).astype(BF16)

        done.append(move(held.at[:, :, columns], out.at[:, :, columns]))

    wait_all(late_x[0])
    update(0)
    wait_all(late_x[1] + late_x[-1])
    update(1)
    update(-1)
    wait_all(late_x[2] + [c for d in (0, -1, 1, 2) for c in late_z[d]])
    update(2)
    for copy in done:
        copy.wait()
    for copy in sent:
        copy.wait_send()


def shards(panel, bases, pivots, ranks, pairs, targets):
    n_tiles, depth, rank = panel.shape
    part = bases.shape[1]
    n_pairs = pairs.shape[0]
    n_rows = lax.axis_size("row")
    group = pltpu.VMEM((SIDE, n_tiles, part, rank), BF16)
    smem = pl.BlockSpec(memory_space=pltpu.SMEM)
    hbm = pl.BlockSpec(memory_space=pl.ANY)
    return pl.pallas_call(
        kernel,
        out_shape=jax.ShapeDtypeStruct(targets.shape, targets.dtype),
        in_specs=[hbm, hbm, smem, smem, smem, hbm],
        out_specs=hbm,
        scratch_shapes=[
            group,
            group,
            group,
            group,
            pltpu.VMEM((n_rows * n_tiles, part, rank), BF16),
            pltpu.VMEM((n_rows * n_tiles, depth, rank), BF16),
            pltpu.VMEM((n_tiles, depth, rank), BF16),
            pltpu.VMEM((SIDE, SIDE, 2, 2, depth, rank), BF16),
            pltpu.VMEM((SIDE, 2, 2, SIDE, depth, rank), BF16),
            pltpu.VMEM((2, 2, SIDE * SIDE, depth, rank), BF16),
            pltpu.VMEM((SIDE, SIDE, 2, rank, rank), BF16),
            pltpu.VMEM((n_pairs, part, rank), BF16),
            pltpu.VMEM(targets.shape, BF16),
            pltpu.VMEM((depth, rank), F32),
            pltpu.SemaphoreType.DMA((80,)),
            pltpu.SemaphoreType.DMA((80,)),
            pltpu.SemaphoreType.DMA((12,)),
        ],
        compiler_params=pltpu.CompilerParams(
            collective_id=0, has_side_effects=True, vmem_limit_bytes=48 << 20
        ),
    )(panel, bases, pivots, ranks, pairs, targets)


def solution(mesh):
    return jax.shard_map(
        shards,
        mesh=mesh,
        in_specs=(
            P("row", "col", None),
            P("row", "col", None),
            P("col"),
            P("row"),
            P("row", None),
            P("row", "col", None),
        ),
        out_specs=P("row", "col", None),
        check_vma=False,
    )
```

```python
import jax
import jax.numpy as jnp
from jax import lax
from jax.experimental import pallas as pl
from jax.experimental.pallas import tpu as pltpu
from jax.sharding import PartitionSpec as P

MESH = pl.DeviceIdType.MESH
F32 = jnp.float32
BF16 = jnp.bfloat16
SIDE = 4


def wrap(v):
    return lax.rem(v + 2 * SIDE, SIDE)


def near(d):
    return (d + 1) % SIDE - 1


def kernel(
    panel, bases, pivot_list, rank_list, pair_list, targets, out,
    pivots, ranks, pairs, here, above, below, across, lefts, tiles, mine, ready, transit, operands, cores, lead, scale,
    send_sem, recv_sem, local_sem,
):
    row = lax.axis_index("row")
    col = lax.axis_index("col")
    y, core = lax.div(row, 2), lax.rem(row, 2)
    z, x = lax.div(col, SIDE), lax.rem(col, SIDE)
    n_tiles, depth, rank = panel.shape
    part = bases.shape[1]
    half = n_tiles // 2
    n_pairs = out.shape[0]
    whole = {0: here, 1: above, -1: below, 2: across}

    def at_col(dz, dx):
        return (row, wrap(z + dz) * SIDE + wrap(x + dx))

    def at_row(dy):
        return (wrap(y + dy) * 2 + core, col)

    twin = (y * 2 + 1 - core, col)

    kept = []

    def move(src, dst):
        copy = pltpu.make_async_copy(src, dst, local_sem.at[len(kept)])
        copy.start()
        kept.append(copy)
        return copy

    own_tiles = pl.ds(row * n_tiles, n_tiles)
    get_ranks = move(rank_list, ranks)
    get_panel = move(panel, mine)
    get_pivots = move(pivot_list, pivots)
    get_pairs = move(pair_list, pairs)
    get_here = move(bases, here.at[x])
    get_left = move(bases, lefts.at[own_tiles])
    get_targets = move(targets, out)

    barrier = pltpu.get_barrier_semaphore()
    friends = [at_col(0, 1), at_col(0, -1), at_col(1, 0), at_col(-1, 0), at_row(1), at_row(-1), twin]
    friends += [at_col(0, 2), at_col(2, 0)]
    for friend in friends:
        pl.semaphore_signal(barrier, inc=1, device_id=friend, device_id_type=MESH)

    get_ranks.wait()
    get_panel.wait()
    lanes = lax.broadcasted_iota(jnp.int32, (depth, rank), 1)

    @pl.loop(0, n_tiles, unroll=4)
    def _(t):
        tile = mine[t].astype(F32)
        tiles[row * n_tiles + t] = jnp.where(lanes < ranks[t], tile, jnp.zeros_like(tile)).astype(BF16)

    get_pivots.wait()
    for r in range(depth):
        scale[pl.ds(r, 1), :] = jnp.full((1, rank), pivots[r], F32)
    get_pairs.wait()
    pl.semaphore_wait(barrier, len(friends))

    sent = []

    def send(src, dst, to):
        k = len(sent)
        copy = pltpu.make_async_remote_copy(
            src_ref=src,
            dst_ref=dst,
            send_sem=send_sem.at[k],
            recv_sem=recv_sem.at[k],
            device_id=to,
            device_id_type=MESH,
        )
        copy.start()
        sent.append(copy)
        return copy

    def pass_on(dz, at_x, to, first, count, fresh=False):
        some = pl.ds(first, count)
        src = bases.at[some] if fresh else whole[near(dz)].at[at_x, some]
        return send(src, whole[near(dz - to[0])].at[at_x, some], at_col(*to))

    def along_x(dz, first, fresh=False):
        return [pass_on(dz, x, (0, d), first, half, fresh) for d in (1, -1)]

    def along_x_far(dz, first, arriving):
        quarter = half // 2
        arriving[0].wait_recv()
        a = pass_on(dz, wrap(x - 1), (0, 1), first, quarter)
        arriving[1].wait_recv()
        b = pass_on(dz, wrap(x + 1), (0, -1), first + quarter, quarter)
        return [a, b]

    def along_z(dx, first, fresh=False):
        return [pass_on(0, wrap(x + dx), (d, 0), first, half, fresh) for d in (1, -1)]

    def along_z_far(dx, first, arriving):
        quarter = half // 2
        arriving[0].wait_recv()
        a = pass_on(-1, wrap(x + dx), (1, 0), first, quarter)
        arriving[1].wait_recv()
        b = pass_on(1, wrap(x + dx), (-1, 0), first + quarter, quarter)
        return [a, b]

    def own_row(array):
        block = array.at[own_tiles]
        return [send(block, block, to) for to in (at_row(1), at_row(-1), twin)]

    def far_row(array, arriving):
        got = []
        for k, d in ((0, -1), (1, 1)):
            first = (wrap(y + d) * 2 + core) * n_tiles
            arriving[k].wait_recv()
            block = array.at[pl.ds(first + k * half, half)]
            got.append(send(block, block, at_row(-d)))
            block = array.at[pl.ds(first, n_tiles)]
            got.append(send(block, block, twin))
        return got

    def last_row(array, arriving):
        first = (wrap(y + 2) * 2 + core) * n_tiles
        got = []
        for k in (0, 1):
            arriving[2 * k].wait_recv()
            block = array.at[pl.ds(first + k * half, half)]
            got.append(send(block, block, twin))
        return got

    def wait_all(copies):
        for copy in copies:
            copy.wait_recv()

    far_x, far_z, first_z, first_x, late_z, late_x = {}, {}, {}, {}, {}, {}
    in_x = along_x(0, 0, True)
    in_z = along_z(0, half, True)
    panel_in = own_row(tiles)
    first_z[0] = along_z(0, 0, True)
    first_x[0] = along_x(0, half, True)
    panel_far = far_row(tiles, panel_in)
    far_x[0] = along_x_far(0, 0, in_x)
    far_z[0] = along_z_far(0, half, in_z)
    get_left.wait()
    left_in = own_row(lefts)
    panel_last = last_row(tiles, panel_far)
    wait_all([panel_in[2], panel_far[1], panel_far[3], *panel_last])

    @pl.loop(0, n_pairs, unroll=4)
    def _(p):
        to = lax.div(p, 2)
        pr, tz, tx = lax.rem(p, 2), lax.div(to, SIDE), lax.rem(to, SIDE)
        scaled = (tiles[pairs[0, p]].astype(F32) * scale[...]).astype(BF16)
        ready[tx, tz, 0, pr] = scaled
        ready[tx, tz, 1, pr] = tiles[pairs[1, p]]

    own_transit = move(ready.at[x], transit.at[:, :, :, x])
    stage_x = [
        send(ready.at[wrap(x + d)], transit.at[:, :, :, x], at_col(0, d)) for d in (1, -1, 2)
    ]

    first_z[1] = along_z(1, 0)
    first_x[1] = along_x(1, half)
    late_z[0] = along_z_far(0, 0, first_z[0])

    own_transit.wait()
    wait_all(stage_x)
    mid = pl.ds(z * SIDE, SIDE)
    own_operands = move(transit.at[z], operands.at[:, :, mid])
    stage_z = [
        send(transit.at[wrap(z + d)], operands.at[:, :, mid], at_col(d, 0)) for d in (1, -1, 2)
    ]

    late_x[0] = along_x_far(0, half, first_x[0])
    first_x[-1] = along_x(-1, half)
    first_z[-1] = along_z(-1, 0)
    left_far = far_row(lefts, left_in)

    own_operands.wait()
    wait_all(stage_z)
    for pr in (0, 1):
        a = operands[0, pr].reshape(SIDE * SIDE * depth, rank)
        b = operands[1, pr].reshape(SIDE * SIDE * depth, rank)
        total = lax.dot_general(a, b, (((0,), (0,)), ((), ())), preferred_element_type=F32)
        cores[z, x, pr] = total.astype(BF16)
    mine_0, mine_1 = cores.at[z, x, 0], cores.at[z, x, 1]
    core_x = [send(mine_0, mine_0, at_col(0, d)) for d in (1, -1, 2)]
    core_z = [send(mine_1, mine_1, at_col(d, 0)) for d in (1, -1, 2)]

    wait_all(far_x[0] + far_z[0])
    first_z[2] = along_z(2, 0)
    first_x[2] = along_x(2, half)
    left_last = last_row(lefts, left_far)

    wait_all(core_x)
    line = cores.at[z, :, 0]
    core_last = [send(line, line, at_col(d, 0)) for d in (1, -1, 2)]
    wait_all(core_z)
    line = cores.at[:, x, 1]
    core_last += [send(line, line, at_col(0, d)) for d in (1, -1, 2)]

    for d in (-1, 1, 2):
        late_z[d] = along_z_far(d, 0, first_z[d])
        late_x[d] = along_x_far(d, half, first_x[d])

    wait_all([left_in[2], left_far[1], left_far[3], *left_last, *core_last])

    @pl.loop(0, n_pairs, unroll=4)
    def _(p):
        to = lax.div(p, 2)
        pr, tz, tx = lax.rem(p, 2), lax.div(to, SIDE), lax.rem(to, SIDE)
        product = jnp.dot(lefts[pairs[0, p]], cores[tz, tx, pr], preferred_element_type=F32)
        lead[p] = product.astype(BF16)

    width = SIDE * part
    get_here.wait()
    get_targets.wait()

    def update(dz):
        group = whole[dz]
        columns = pl.ds(pl.multiple_of(wrap(z + dz) * width, width), width)

        @pl.loop(0, n_pairs, unroll=8)
        def _(p):
            right = group[:, lax.rem(pairs[1, p], n_tiles)].reshape(width, rank)
            change = lax.dot_general(
                lead[p], right, (((1,), (1,)), ((), ())), preferred_element_type=F32
            )
            out[p, :, columns] = (out[p, :, columns].astype(F32) - change).astype(BF16)

    wait_all(late_x[0])
    update(0)
    wait_all(late_x[1] + late_x[-1])
    update(1)
    update(-1)
    wait_all(late_x[2] + [c for d in (0, -1, 1, 2) for c in late_z[d]])
    update(2)
    for copy in sent:
        copy.wait_send()


def shards(panel, bases, pivots, ranks, pairs, targets):
    n_tiles, depth, rank = panel.shape
    part = bases.shape[1]
    n_pairs = pairs.shape[0]
    n_rows = lax.axis_size("row")
    group = pltpu.VMEM((SIDE, n_tiles, part, rank), BF16)
    hbm = pl.BlockSpec(memory_space=pltpu.HBM)
    return pl.pallas_call(
        kernel,
        out_shape=jax.ShapeDtypeStruct(targets.shape, targets.dtype),
        in_specs=[hbm] * 6,
        out_specs=pl.BlockSpec(memory_space=pltpu.VMEM),
        scratch_shapes=[
            pltpu.SMEM(pivots.shape, F32),
            pltpu.SMEM(ranks.shape, jnp.int32),
            pltpu.SMEM((2, n_pairs), jnp.int32),
            group,
            group,
            group,
            group,
            pltpu.VMEM((n_rows * n_tiles, part, rank), BF16),
            pltpu.VMEM((n_rows * n_tiles, depth, rank), BF16),
            pltpu.VMEM((n_tiles, depth, rank), BF16),
            pltpu.VMEM((SIDE, SIDE, 2, 2, depth, rank), BF16),
            pltpu.VMEM((SIDE, 2, 2, SIDE, depth, rank), BF16),
            pltpu.VMEM((2, 2, SIDE * SIDE, depth, rank), BF16),
            pltpu.VMEM((SIDE, SIDE, 2, rank, rank), BF16),
            pltpu.VMEM((n_pairs, part, rank), BF16),
            pltpu.VMEM((depth, rank), F32),
            pltpu.SemaphoreType.DMA((80,)),
            pltpu.SemaphoreType.DMA((80,)),
            pltpu.SemaphoreType.DMA((12,)),
        ],
        compiler_params=pltpu.CompilerParams(
            collective_id=0, has_side_effects=True, vmem_limit_bytes=48 << 20
        ),
    )(*(pltpu.with_memory_space_constraint(a, pltpu.HBM) for a in (panel, bases, pivots, ranks, pairs.T, targets)))


def solution(mesh):
    return jax.shard_map(
        shards,
        mesh=mesh,
        in_specs=(
            P("row", "col", None),
            P("row", "col", None),
            P("col"),
            P("row"),
            P("row", None),
            P("row", "col", None),
        ),
        out_specs=P("row", "col", None),
        check_vma=False,
    )
```

```python
import jax
import jax.numpy as jnp
from jax import lax
from jax.experimental import pallas as pl
from jax.experimental.pallas import tpu as pltpu
from jax.sharding import PartitionSpec as P

MESH = pl.DeviceIdType.MESH
F32 = jnp.float32
BF16 = jnp.bfloat16
SIDE = 4


def wrap(v):
    return lax.rem(v + 2 * SIDE, SIDE)


def near(d):
    return (d + 1) % SIDE - 1


def kernel(
    panel, bases, pivot_list, rank_list, pair_list, targets, out,
    pivots, ranks, pairs, here, above, below, across, lefts, tiles, mine, ready, transit, partial, arrived, cores, lead, scale,
    send_sem, recv_sem, local_sem,
):
    row = lax.axis_index("row")
    col = lax.axis_index("col")
    y, core = lax.div(row, 2), lax.rem(row, 2)
    z, x = lax.div(col, SIDE), lax.rem(col, SIDE)
    n_tiles, depth, rank = panel.shape
    part = bases.shape[1]
    half = n_tiles // 2
    n_pairs = out.shape[0]
    whole = {0: here, 1: above, -1: below, 2: across}

    def at_col(dz, dx):
        return (row, wrap(z + dz) * SIDE + wrap(x + dx))

    def at_row(dy):
        return (wrap(y + dy) * 2 + core, col)

    twin = (y * 2 + 1 - core, col)

    barrier = pltpu.get_barrier_semaphore()
    friends = [at_col(0, 1), at_col(0, -1), at_col(1, 0), at_col(-1, 0), at_row(1), at_row(-1), twin]
    friends += [at_col(0, 2), at_col(2, 0)]
    for friend in friends:
        pl.semaphore_signal(barrier, inc=1, device_id=friend, device_id_type=MESH)

    kept = []

    def move(src, dst):
        copy = pltpu.make_async_copy(src, dst, local_sem.at[len(kept)])
        copy.start()
        kept.append(copy)
        return copy

    own_tiles = pl.ds(row * n_tiles, n_tiles)
    get_ranks = move(rank_list, ranks)
    get_panel = move(panel, mine)
    get_pivots = move(pivot_list, pivots)
    get_pairs = move(pair_list, pairs)
    get_here = move(bases, here.at[x])
    get_left = move(bases, lefts.at[own_tiles])
    get_targets = move(targets, out)

    pl.semaphore_wait(barrier, len(friends))

    sent = []

    def send(src, dst, to):
        k = len(sent)
        copy = pltpu.make_async_remote_copy(
            src_ref=src,
            dst_ref=dst,
            send_sem=send_sem.at[k],
            recv_sem=recv_sem.at[k],
            device_id=to,
            device_id_type=MESH,
        )
        copy.start()
        sent.append(copy)
        return copy

    def pass_on(dz, at_x, to, first, count, fresh=False):
        some = pl.ds(first, count)
        src = bases.at[some] if fresh else whole[near(dz)].at[at_x, some]
        return send(src, whole[near(dz - to[0])].at[at_x, some], at_col(*to))

    def along_x(dz, first, fresh=False, count=half):
        return [pass_on(dz, x, (0, d), first, count, fresh) for d in (1, -1)]

    def along_x_far(dz, first, arriving):
        quarter = half // 2
        arriving[0].wait_recv()
        a = pass_on(dz, wrap(x - 1), (0, 1), first, quarter)
        arriving[1].wait_recv()
        b = pass_on(dz, wrap(x + 1), (0, -1), first + quarter, quarter)
        return [a, b]

    def along_z(dx, first, fresh=False, count=half):
        return [pass_on(0, wrap(x + dx), (d, 0), first, count, fresh) for d in (1, -1)]

    def along_z_far(dx, first, arriving):
        quarter = half // 2
        arriving[0].wait_recv()
        a = pass_on(-1, wrap(x + dx), (1, 0), first, quarter)
        arriving[1].wait_recv()
        b = pass_on(1, wrap(x + dx), (-1, 0), first + quarter, quarter)
        return [a, b]

    def own_row(array):
        block = array.at[own_tiles]
        return [send(block, block, to) for to in (at_row(1), at_row(-1), twin)]

    def far_row(array, arriving):
        got = []
        for k, d in ((0, -1), (1, 1)):
            first = (wrap(y + d) * 2 + core) * n_tiles
            arriving[k].wait_recv()
            block = array.at[pl.ds(first + k * half, half)]
            got.append(send(block, block, at_row(-d)))
            block = array.at[pl.ds(first, n_tiles)]
            got.append(send(block, block, twin))
        return got

    def last_row(array, arriving):
        first = (wrap(y + 2) * 2 + core) * n_tiles
        got = []
        for k in (0, 1):
            arriving[2 * k].wait_recv()
            block = array.at[pl.ds(first + k * half, half)]
            got.append(send(block, block, twin))
        return got

    def wait_all(copies):
        for copy in copies:
            copy.wait_recv()

    far_x, far_z, first_z, first_x, late_z, late_x = {}, {}, {}, {}, {}, {}
    in_x = along_x(0, 0, True)
    in_z = along_z(0, half, True)
    first_z[0] = along_z(0, 0, True)
    first_x[0] = along_x(0, half, True)

    get_ranks.wait()
    get_panel.wait()
    lanes = lax.broadcasted_iota(jnp.int32, (depth, rank), 1)

    @pl.loop(0, n_tiles, unroll=4)
    def _(t):
        tile = mine[t].astype(F32)
        tiles[row * n_tiles + t] = jnp.where(lanes < ranks[t], tile, jnp.zeros_like(tile)).astype(BF16)

    get_pivots.wait()
    for r in range(depth):
        scale[pl.ds(r, 1), :] = jnp.full((1, rank), pivots[r], F32)

    panel_in = own_row(tiles)
    panel_far = far_row(tiles, panel_in)
    far_x[0] = along_x_far(0, 0, in_x)
    far_z[0] = along_z_far(0, half, in_z)
    some_z = along_z(1, 0, count=half // 2)
    some_x = along_x(1, half, count=half // 2)
    get_left.wait()
    left_in = own_row(lefts)
    panel_last = last_row(tiles, panel_far)
    get_pairs.wait()
    wait_all([panel_in[2], panel_far[1], panel_far[3], *panel_last])

    @pl.loop(0, n_pairs // 2, unroll=2)
    def _(to):
        tz, tx = lax.div(to, SIDE), lax.rem(to, SIDE)
        for pr, a, b in ((0, tx, tz), (1, tz, tx)):
            left, right = pairs[0, 2 * to + pr], pairs[1, 2 * to + pr]
            ready[pr, a, b, 0] = (tiles[left].astype(F32) * scale[...]).astype(BF16)
            ready[pr, a, b, 1] = tiles[right]

    place = (x, z)
    step = (lambda d: at_col(0, d), lambda d: at_col(d, 0))
    own_transit, operands_in = [], []
    for pr in (0, 1):
        me = transit.at[pr, :, :, place[pr]]
        own_transit.append(move(ready.at[pr, place[pr]], me))
        for d in (1, -1, 2):
            operands_in.append(send(ready.at[pr, wrap(place[pr] + d)], me, step[pr](d)))

    late_z[0] = along_z_far(0, 0, first_z[0])
    late_x[0] = along_x_far(0, half, first_x[0])

    for copy in own_transit:
        copy.wait()
    wait_all(operands_in)

    def partial_sum(pr, at):
        a = transit[pr, at, 0].reshape(SIDE * depth, rank)
        b = transit[pr, at, 1].reshape(SIDE * depth, rank)
        return lax.dot_general(a, b, (((0,), (0,)), ((), ())), preferred_element_type=F32)

    partials_in = []
    for pr in (0, 1):
        at = place[1 - pr]
        for d in (1, -1, 2):
            there = wrap(at + d)
            partial[pr, there] = partial_sum(pr, there).astype(BF16)
            partials_in.append(send(partial.at[pr, there], arrived.at[pr, at], step[1 - pr](d)))

    rest_z = along_z(1, half // 2, count=half // 2)
    rest_x = along_x(1, half + half // 2, count=half // 2)
    first_z[1] = [some_z[0], rest_z[1]]
    first_x[1] = [some_x[0], rest_x[1]]
    totals = [partial_sum(pr, place[1 - pr]) for pr in (0, 1)]
    wait_all(partials_in)
    for pr in (0, 1):
        total = totals[pr]
        for d in (1, 2, 3):
            total = total + arrived[pr, wrap(place[1 - pr] + d)].astype(F32)
        cores[z, x, pr] = total.astype(BF16)
    core_in = []
    for pr in (0, 1):
        block = cores.at[z, x, pr]
        core_in.append([send(block, block, step[pr](d)) for d in (1, -1, 2)])

    first_z[-1] = along_z(-1, 0)
    first_x[-1] = along_x(-1, half)
    left_far = far_row(lefts, left_in)

    def line(pr, d, first, count):
        some = pl.ds(first, count)
        if pr == 0:
            return cores.at[wrap(z + d), some, 0]
        return cores.at[some, wrap(x + d), 1]

    line_in, line_far = [], []
    for pr in (0, 1):
        wait_all(core_in[pr])
        block = line(pr, 0, 0, SIDE)
        line_in.append([send(block, block, step[1 - pr](d)) for d in (1, -1)])

    wait_all(far_x[0] + far_z[0])
    first_z[2] = along_z(2, 0)
    first_x[2] = along_x(2, half)
    left_last = last_row(lefts, left_far)
    for pr in (0, 1):
        for k, d in ((0, 1), (1, -1)):
            line_in[pr][k].wait_recv()
            block = line(pr, -d, k * SIDE // 2, SIDE // 2)
            line_far.append(send(block, block, step[1 - pr](d)))

    for d in (-1, 1, 2):
        late_z[d] = along_z_far(d, 0, first_z[d])
        late_x[d] = along_x_far(d, half, first_x[d])

    wait_all([left_in[2], left_far[1], left_far[3], *left_last, *line_far])

    @pl.loop(0, n_pairs, unroll=4)
    def _(p):
        to = lax.div(p, 2)
        pr, tz, tx = lax.rem(p, 2), lax.div(to, SIDE), lax.rem(to, SIDE)
        product = jnp.dot(lefts[pairs[0, p]], cores[tz, tx, pr], preferred_element_type=F32)
        lead[p] = product.astype(BF16)

    width = SIDE * part
    get_here.wait()
    get_targets.wait()

    def update(dz):
        group = whole[dz]
        columns = pl.ds(pl.multiple_of(wrap(z + dz) * width, width), width)

        @pl.loop(0, n_pairs, unroll=16)
        def _(p):
            right = group[:, lax.rem(pairs[1, p], n_tiles)].reshape(width, rank)
            change = lax.dot_general(
                lead[p], right, (((1,), (1,)), ((), ())), preferred_element_type=F32
            )
            out[p, :, columns] = (out[p, :, columns].astype(F32) - change).astype(BF16)

    wait_all(late_x[0])
    update(0)
    wait_all([some_x[1], rest_x[0], some_z[1], rest_z[0]])
    wait_all(late_x[1] + late_x[-1])
    update(1)
    update(-1)
    wait_all(late_x[2] + [c for d in (0, -1, 1, 2) for c in late_z[d]])
    update(2)
    for copy in sent:
        copy.wait_send()


def shards(panel, bases, pivots, ranks, pairs, targets):
    n_tiles, depth, rank = panel.shape
    part = bases.shape[1]
    n_pairs = pairs.shape[0]
    n_rows = lax.axis_size("row")
    group = pltpu.VMEM((SIDE, n_tiles, part, rank), BF16)
    hbm = pl.BlockSpec(memory_space=pltpu.HBM)
    return pl.pallas_call(
        kernel,
        out_shape=jax.ShapeDtypeStruct(targets.shape, targets.dtype),
        in_specs=[hbm] * 6,
        out_specs=pl.BlockSpec(memory_space=pltpu.VMEM),
        scratch_shapes=[
            pltpu.SMEM(pivots.shape, F32),
            pltpu.SMEM(ranks.shape, jnp.int32),
            pltpu.SMEM((2, n_pairs), jnp.int32),
            group,
            group,
            group,
            group,
            pltpu.VMEM((n_rows * n_tiles, part, rank), BF16),
            pltpu.VMEM((n_rows * n_tiles, depth, rank), BF16),
            pltpu.VMEM((n_tiles, depth, rank), BF16),
            pltpu.VMEM((2, SIDE, SIDE, 2, depth, rank), BF16),
            pltpu.VMEM((2, SIDE, 2, SIDE, depth, rank), BF16),
            pltpu.VMEM((2, SIDE, rank, rank), BF16),
            pltpu.VMEM((2, SIDE, rank, rank), BF16),
            pltpu.VMEM((SIDE, SIDE, 2, rank, rank), BF16),
            pltpu.VMEM((n_pairs, part, rank), BF16),
            pltpu.VMEM((depth, rank), F32),
            pltpu.SemaphoreType.DMA((92,)),
            pltpu.SemaphoreType.DMA((92,)),
            pltpu.SemaphoreType.DMA((12,)),
        ],
        compiler_params=pltpu.CompilerParams(
            collective_id=0, has_side_effects=True, vmem_limit_bytes=48 << 20
        ),
    )(*(pltpu.with_memory_space_constraint(a, pltpu.HBM) for a in (panel, bases, pivots, ranks, pairs.T, targets)))


def solution(mesh):
    return jax.shard_map(
        shards,
        mesh=mesh,
        in_specs=(
            P("row", "col", None),
            P("row", "col", None),
            P("col"),
            P("row"),
            P("row", None),
            P("row", "col", None),
        ),
        out_specs=P("row", "col", None),
        check_vma=False,
    )
```

```python
import jax
import jax.numpy as jnp
from jax import lax
from jax.experimental import pallas as pl
from jax.experimental.pallas import tpu as pltpu
from jax.sharding import PartitionSpec as P

MESH = pl.DeviceIdType.MESH
F32 = jnp.float32
BF16 = jnp.bfloat16
SIDE = 4


def wrap(v):
    return lax.rem(v + 2 * SIDE, SIDE)


def near(d):
    return (d + 1) % SIDE - 1


def kernel(
    panel, bases, pivot_list, rank_list, pair_list, targets, out,
    pivots, ranks, pairs, here, above, below, across, lefts, tiles, mine, ready, transit, partial, arrived, cores, lead, scale,
    send_sem, recv_sem, local_sem,
):
    row = lax.axis_index("row")
    col = lax.axis_index("col")
    y, core = lax.div(row, 2), lax.rem(row, 2)
    z, x = lax.div(col, SIDE), lax.rem(col, SIDE)
    n_tiles, depth, rank = panel.shape
    part = bases.shape[1]
    half = n_tiles // 2
    n_pairs = out.shape[0]
    whole = {0: here, 1: above, -1: below, 2: across}

    def at_col(dz, dx):
        return (row, wrap(z + dz) * SIDE + wrap(x + dx))

    def at_row(dy):
        return (wrap(y + dy) * 2 + core, col)

    twin = (y * 2 + 1 - core, col)

    barrier = pltpu.get_barrier_semaphore()
    friends = [at_col(0, 1), at_col(0, -1), at_col(1, 0), at_col(-1, 0), at_row(1), at_row(-1), twin]
    friends += [at_col(0, 2), at_col(2, 0)]
    for friend in friends:
        pl.semaphore_signal(barrier, inc=1, device_id=friend, device_id_type=MESH)

    kept = []

    def move(src, dst):
        copy = pltpu.make_async_copy(src, dst, local_sem.at[len(kept)])
        copy.start()
        kept.append(copy)
        return copy

    own_tiles = pl.ds(row * n_tiles, n_tiles)
    get_ranks = move(rank_list, ranks)
    get_panel = move(panel, mine)
    get_pivots = move(pivot_list, pivots)
    get_pairs = move(pair_list, pairs)
    get_here = move(bases, here.at[x])
    get_left = move(bases, lefts.at[own_tiles])
    get_targets = move(targets, out)

    pl.semaphore_wait(barrier, len(friends))

    sent = []

    def send(src, dst, to):
        k = len(sent)
        copy = pltpu.make_async_remote_copy(
            src_ref=src,
            dst_ref=dst,
            send_sem=send_sem.at[k],
            recv_sem=recv_sem.at[k],
            device_id=to,
            device_id_type=MESH,
        )
        copy.start()
        sent.append(copy)
        return copy

    def pass_on(dz, at_x, to, first, count, fresh=False):
        some = pl.ds(first, count)
        src = bases.at[some] if fresh else whole[near(dz)].at[at_x, some]
        return send(src, whole[near(dz - to[0])].at[at_x, some], at_col(*to))

    def along_x(dz, first, fresh=False, count=half):
        return [pass_on(dz, x, (0, d), first, count, fresh) for d in (1, -1)]

    def along_x_far(dz, first, arriving):
        quarter = half // 2
        arriving[0].wait_recv()
        a = pass_on(dz, wrap(x - 1), (0, 1), first, quarter)
        arriving[1].wait_recv()
        b = pass_on(dz, wrap(x + 1), (0, -1), first + quarter, quarter)
        return [a, b]

    def along_z(dx, first, fresh=False, count=half):
        return [pass_on(0, wrap(x + dx), (d, 0), first, count, fresh) for d in (1, -1)]

    def along_z_far(dx, first, arriving):
        quarter = half // 2
        arriving[0].wait_recv()
        a = pass_on(-1, wrap(x + dx), (1, 0), first, quarter)
        arriving[1].wait_recv()
        b = pass_on(1, wrap(x + dx), (-1, 0), first + quarter, quarter)
        return [a, b]

    def own_row(array):
        got = []
        for k, d in ((0, 1), (1, -1), (1, 1), (0, -1)):
            block = array.at[pl.ds(row * n_tiles + k * half, half)]
            got.append(send(block, block, at_row(d)))
        block = array.at[own_tiles]
        return got + [send(block, block, twin)]

    def far_row(array, arriving):
        got, seen = [], []
        for k, d in ((0, 1), (1, -1), (1, 1), (0, -1)):
            first = (wrap(y - d) * 2 + core) * n_tiles + k * half
            arriving[len(seen)].wait_recv()
            block = array.at[pl.ds(first, half)]
            seen.append(block)
            if len(seen) <= 2:
                got.append(send(block, block, at_row(d)))
        return got + [send(block, block, twin) for block in seen]

    def last_row(array, arriving):
        first = (wrap(y + 2) * 2 + core) * n_tiles
        got = []
        for k in (0, 1):
            arriving[k].wait_recv()
            block = array.at[pl.ds(first + k * half, half)]
            got.append(send(block, block, twin))
        return got

    def wait_all(copies):
        for copy in copies:
            copy.wait_recv()

    far_x, far_z, first_z, first_x, late_z, late_x = {}, {}, {}, {}, {}, {}
    in_x = along_x(0, 0, True)
    in_z = along_z(0, half, True)
    first_z[0] = along_z(0, 0, True)
    first_x[0] = along_x(0, half, True)

    get_ranks.wait()
    get_panel.wait()
    lanes = lax.broadcasted_iota(jnp.int32, (depth, rank), 1)

    @pl.loop(0, n_tiles, unroll=4)
    def _(t):
        tile = mine[t].astype(F32)
        tiles[row * n_tiles + t] = jnp.where(lanes < ranks[t], tile, jnp.zeros_like(tile)).astype(BF16)

    get_pivots.wait()
    for r in range(depth):
        scale[pl.ds(r, 1), :] = jnp.full((1, rank), pivots[r], F32)

    panel_in = own_row(tiles)
    panel_far = far_row(tiles, panel_in)
    far_x[0] = along_x_far(0, 0, in_x)
    far_z[0] = along_z_far(0, half, in_z)
    get_left.wait()
    left_in = own_row(lefts)
    panel_last = last_row(tiles, panel_far)
    get_pairs.wait()
    wait_all([panel_in[4], *panel_far[2:], *panel_last])

    @pl.loop(0, n_pairs // 2, unroll=2)
    def _(to):
        tz, tx = lax.div(to, SIDE), lax.rem(to, SIDE)
        for pr, a, b in ((0, tx, tz), (1, tz, tx)):
            left, right = pairs[0, 2 * to + pr], pairs[1, 2 * to + pr]
            ready[pr, a, b, 0] = (tiles[left].astype(F32) * scale[...]).astype(BF16)
            ready[pr, a, b, 1] = tiles[right]

    place = (x, z)
    step = (lambda d: at_col(0, d), lambda d: at_col(d, 0))
    own_transit, operands_in = [], []
    for pr in (0, 1):
        me = transit.at[pr, :, :, place[pr]]
        own_transit.append(move(ready.at[pr, place[pr]], me))
        for d in (1, -1, 2):
            operands_in.append(send(ready.at[pr, wrap(place[pr] + d)], me, step[pr](d)))

    late_z[0] = along_z_far(0, 0, first_z[0])
    late_x[0] = along_x_far(0, half, first_x[0])
    some_z = along_z(1, 0, count=half // 2)
    some_x = along_x(1, half, count=half // 2)

    for copy in own_transit:
        copy.wait()
    wait_all(operands_in)

    def partial_sum(pr, at):
        a = transit[pr, at, 0].reshape(SIDE * depth, rank)
        b = transit[pr, at, 1].reshape(SIDE * depth, rank)
        return lax.dot_general(a, b, (((0,), (0,)), ((), ())), preferred_element_type=F32)

    partials_in = []
    for pr in (0, 1):
        at = place[1 - pr]
        for d in (1, -1, 2):
            there = wrap(at + d)
            partial[pr, there] = partial_sum(pr, there).astype(BF16)
            partials_in.append(send(partial.at[pr, there], arrived.at[pr, at], step[1 - pr](d)))

    rest_z = along_z(1, half // 2, count=half // 2)
    rest_x = along_x(1, half + half // 2, count=half // 2)
    first_z[1] = [some_z[0], rest_z[1]]
    first_x[1] = [some_x[0], rest_x[1]]
    totals = [partial_sum(pr, place[1 - pr]) for pr in (0, 1)]
    wait_all(partials_in)
    for pr in (0, 1):
        total = totals[pr]
        for d in (1, 2, 3):
            total = total + arrived[pr, wrap(place[1 - pr] + d)].astype(F32)
        cores[z, x, pr] = total.astype(BF16)
    core_in = []
    for pr in (0, 1):
        block = cores.at[z, x, pr]
        core_in.append([send(block, block, step[pr](d)) for d in (1, -1, 2)])

    first_z[-1] = along_z(-1, 0)
    first_x[-1] = along_x(-1, half)
    left_far = far_row(lefts, left_in)

    def line(pr, d, first, count):
        some = pl.ds(first, count)
        if pr == 0:
            return cores.at[wrap(z + d), some, 0]
        return cores.at[some, wrap(x + d), 1]

    line_in, line_far = [], []
    for pr in (0, 1):
        wait_all(core_in[pr])
        block = line(pr, 0, 0, SIDE)
        line_in.append([send(block, block, step[1 - pr](d)) for d in (1, -1)])

    wait_all(far_x[0] + far_z[0])
    first_z[2] = along_z(2, 0)
    first_x[2] = along_x(2, half)
    left_last = last_row(lefts, left_far)
    for pr in (0, 1):
        for k, d in ((0, 1), (1, -1)):
            line_in[pr][k].wait_recv()
            block = line(pr, -d, k * SIDE // 2, SIDE // 2)
            line_far.append(send(block, block, step[1 - pr](d)))

    for d in (-1, 1, 2):
        late_z[d] = along_z_far(d, 0, first_z[d])
        late_x[d] = along_x_far(d, half, first_x[d])

    wait_all([left_in[4], *left_far[2:], *left_last, *line_far])

    @pl.loop(0, n_pairs, unroll=4)
    def _(p):
        to = lax.div(p, 2)
        pr, tz, tx = lax.rem(p, 2), lax.div(to, SIDE), lax.rem(to, SIDE)
        product = jnp.dot(lefts[pairs[0, p]], cores[tz, tx, pr], preferred_element_type=F32)
        lead[p] = product.astype(BF16)

    width = SIDE * part
    get_here.wait()
    get_targets.wait()

    def update(dz):
        group = whole[dz]
        columns = pl.ds(pl.multiple_of(wrap(z + dz) * width, width), width)

        @pl.loop(0, n_pairs, unroll=32)
        def _(p):
            right = group[:, lax.rem(pairs[1, p], n_tiles)].reshape(width, rank)
            change = lax.dot_general(
                lead[p], right, (((1,), (1,)), ((), ())), preferred_element_type=F32
            )
            out[p, :, columns] = (out[p, :, columns].astype(F32) - change).astype(BF16)

    wait_all(late_x[0])
    update(0)
    wait_all([some_x[1], rest_x[0], some_z[1], rest_z[0]])
    wait_all(late_x[1] + late_x[-1])
    update(1)
    update(-1)
    wait_all(late_x[2] + [c for d in (0, -1, 1, 2) for c in late_z[d]])
    update(2)
    for copy in sent:
        copy.wait_send()


def shards(panel, bases, pivots, ranks, pairs, targets):
    n_tiles, depth, rank = panel.shape
    part = bases.shape[1]
    n_pairs = pairs.shape[0]
    n_rows = lax.axis_size("row")
    group = pltpu.VMEM((SIDE, n_tiles, part, rank), BF16)
    hbm = pl.BlockSpec(memory_space=pltpu.HBM)
    return pl.pallas_call(
        kernel,
        out_shape=jax.ShapeDtypeStruct(targets.shape, targets.dtype),
        in_specs=[hbm] * 6,
        out_specs=pl.BlockSpec(memory_space=pltpu.VMEM),
        scratch_shapes=[
            pltpu.SMEM(pivots.shape, F32),
            pltpu.SMEM(ranks.shape, jnp.int32),
            pltpu.SMEM((2, n_pairs), jnp.int32),
            group,
            group,
            group,
            group,
            pltpu.VMEM((n_rows * n_tiles, part, rank), BF16),
            pltpu.VMEM((n_rows * n_tiles, depth, rank), BF16),
            pltpu.VMEM((n_tiles, depth, rank), BF16),
            pltpu.VMEM((2, SIDE, SIDE, 2, depth, rank), BF16),
            pltpu.VMEM((2, SIDE, 2, SIDE, depth, rank), BF16),
            pltpu.VMEM((2, SIDE, rank, rank), BF16),
            pltpu.VMEM((2, SIDE, rank, rank), BF16),
            pltpu.VMEM((SIDE, SIDE, 2, rank, rank), BF16),
            pltpu.VMEM((n_pairs, part, rank), BF16),
            pltpu.VMEM((depth, rank), F32),
            pltpu.SemaphoreType.DMA((100,)),
            pltpu.SemaphoreType.DMA((100,)),
            pltpu.SemaphoreType.DMA((12,)),
        ],
        compiler_params=pltpu.CompilerParams(
            collective_id=0, has_side_effects=True, vmem_limit_bytes=48 << 20
        ),
    )(*(pltpu.with_memory_space_constraint(a, pltpu.HBM) for a in (panel, bases, pivots, ranks, pairs.T, targets)))


def solution(mesh):
    return jax.shard_map(
        shards,
        mesh=mesh,
        in_specs=(
            P("row", "col", None),
            P("row", "col", None),
            P("col"),
            P("row"),
            P("row", None),
            P("row", "col", None),
        ),
        out_specs=P("row", "col", None),
        check_vma=False,
    )
```

```python
import jax
import jax.numpy as jnp
from jax import lax
from jax.experimental import pallas as pl
from jax.experimental.pallas import tpu as pltpu
from jax.sharding import PartitionSpec as P

MESH = pl.DeviceIdType.MESH
F32 = jnp.float32
BF16 = jnp.bfloat16
SIDE = 4


def wrap(v):
    return lax.rem(v + 2 * SIDE, SIDE)


def near(d):
    return (d + 1) % SIDE - 1


def kernel(
    panel, bases, pivot_list, rank_list, pair_list, targets, out,
    pivots, ranks, pairs, here, above, below, across, lefts, tiles, mine, ready, transit, partial, arrived, cores, lead, scale,
    send_sem, recv_sem, local_sem,
):
    row = lax.axis_index("row")
    col = lax.axis_index("col")
    y, core = lax.div(row, 2), lax.rem(row, 2)
    z, x = lax.div(col, SIDE), lax.rem(col, SIDE)
    n_tiles, depth, rank = panel.shape
    part = bases.shape[1]
    half = n_tiles // 2
    n_pairs = out.shape[0]
    whole = {0: here, 1: above, -1: below, 2: across}

    def at_col(dz, dx):
        return (row, wrap(z + dz) * SIDE + wrap(x + dx))

    def at_row(dy):
        return (wrap(y + dy) * 2 + core, col)

    twin = (y * 2 + 1 - core, col)

    barrier = pltpu.get_barrier_semaphore()
    friends = [at_col(0, 1), at_col(0, -1), at_col(1, 0), at_col(-1, 0), at_row(1), at_row(-1), twin]
    friends += [at_col(0, 2), at_col(2, 0)]
    for friend in friends:
        pl.semaphore_signal(barrier, inc=1, device_id=friend, device_id_type=MESH)

    kept = []

    def move(src, dst):
        copy = pltpu.make_async_copy(src, dst, local_sem.at[len(kept)])
        copy.start()
        kept.append(copy)
        return copy

    own_tiles = pl.ds(row * n_tiles, n_tiles)
    get_ranks = move(rank_list, ranks)
    get_panel = move(panel, mine)
    get_pivots = move(pivot_list, pivots)
    get_pairs = move(pair_list, pairs)
    get_here = move(bases, here.at[x])
    get_left = move(bases, lefts.at[own_tiles])
    get_targets = move(targets, out)

    pl.semaphore_wait(barrier, len(friends))

    sent = []

    def send(src, dst, to):
        k = len(sent)
        copy = pltpu.make_async_remote_copy(
            src_ref=src,
            dst_ref=dst,
            send_sem=send_sem.at[k],
            recv_sem=recv_sem.at[k],
            device_id=to,
            device_id_type=MESH,
        )
        copy.start()
        sent.append(copy)
        return copy

    def pass_on(dz, at_x, to, first, count, fresh=False):
        some = pl.ds(first, count)
        src = bases.at[some] if fresh else whole[near(dz)].at[at_x, some]
        return send(src, whole[near(dz - to[0])].at[at_x, some], at_col(*to))

    def along_x(dz, first, fresh=False, count=half):
        return [pass_on(dz, x, (0, d), first, count, fresh) for d in (1, -1)]

    def along_x_far(dz, first, arriving):
        quarter = half // 2
        arriving[0].wait_recv()
        a = pass_on(dz, wrap(x - 1), (0, 1), first, quarter)
        arriving[1].wait_recv()
        b = pass_on(dz, wrap(x + 1), (0, -1), first + quarter, quarter)
        return [a, b]

    def along_z(dx, first, fresh=False, count=half):
        return [pass_on(0, wrap(x + dx), (d, 0), first, count, fresh) for d in (1, -1)]

    def along_z_far(dx, first, arriving):
        quarter = half // 2
        arriving[0].wait_recv()
        a = pass_on(-1, wrap(x + dx), (1, 0), first, quarter)
        arriving[1].wait_recv()
        b = pass_on(1, wrap(x + dx), (-1, 0), first + quarter, quarter)
        return [a, b]

    def own_row(array):
        got = []
        for k, d in ((0, 1), (1, -1), (1, 1), (0, -1)):
            block = array.at[pl.ds(row * n_tiles + k * half, half)]
            got.append(send(block, block, at_row(d)))
        block = array.at[own_tiles]
        return got + [send(block, block, twin)]

    def far_row(array, arriving):
        got, seen = [], []
        for k, d in ((0, 1), (1, -1), (1, 1), (0, -1)):
            first = (wrap(y - d) * 2 + core) * n_tiles + k * half
            arriving[len(seen)].wait_recv()
            block = array.at[pl.ds(first, half)]
            seen.append(block)
            if len(seen) <= 2:
                got.append(send(block, block, at_row(d)))
        return got + [send(block, block, twin) for block in seen]

    def last_row(array, arriving):
        first = (wrap(y + 2) * 2 + core) * n_tiles
        got = []
        for k in (0, 1):
            arriving[k].wait_recv()
            block = array.at[pl.ds(first + k * half, half)]
            got.append(send(block, block, twin))
        return got

    def wait_all(copies):
        for copy in copies:
            copy.wait_recv()

    far_x, far_z, first_z, first_x, late_z, late_x = {}, {}, {}, {}, {}, {}
    in_x = along_x(0, 0, True)
    in_z = along_z(0, half, True)

    get_ranks.wait()
    get_panel.wait()
    lanes = lax.broadcasted_iota(jnp.int32, (depth, rank), 1)

    @pl.loop(0, n_tiles, unroll=4)
    def _(t):
        tile = mine[t].astype(F32)
        tiles[row * n_tiles + t] = jnp.where(lanes < ranks[t], tile, jnp.zeros_like(tile)).astype(BF16)


    panel_in = own_row(tiles)
    first_z[0] = along_z(0, 0, True)
    first_x[0] = along_x(0, half, True)
    get_pivots.wait()
    for r in range(depth):
        scale[pl.ds(r, 1), :] = jnp.full((1, rank), pivots[r], F32)
    panel_far = far_row(tiles, panel_in)
    far_x[0] = along_x_far(0, 0, in_x)
    far_z[0] = along_z_far(0, half, in_z)
    get_left.wait()
    left_in = own_row(lefts)
    panel_last = last_row(tiles, panel_far)
    get_pairs.wait()
    wait_all([panel_in[4], *panel_far[2:], *panel_last])

    @pl.loop(0, n_pairs // 2, unroll=2)
    def _(to):
        tz, tx = lax.div(to, SIDE), lax.rem(to, SIDE)
        for pr, a, b in ((0, tx, tz), (1, tz, tx)):
            left, right = pairs[0, 2 * to + pr], pairs[1, 2 * to + pr]
            ready[pr, a, b, 0] = (tiles[left].astype(F32) * scale[...]).astype(BF16)
            ready[pr, a, b, 1] = tiles[right]

    place = (x, z)
    step = (lambda d: at_col(0, d), lambda d: at_col(d, 0))
    own_transit, operands_in = [], []
    for pr in (0, 1):
        me = transit.at[pr, :, :, place[pr]]
        own_transit.append(move(ready.at[pr, place[pr]], me))
        for d in (1, -1, 2):
            operands_in.append(send(ready.at[pr, wrap(place[pr] + d)], me, step[pr](d)))

    late_z[0] = along_z_far(0, 0, first_z[0])
    late_x[0] = along_x_far(0, half, first_x[0])
    some_z = along_z(1, 0, count=half // 2)
    some_x = along_x(1, half, count=half // 2)

    for copy in own_transit:
        copy.wait()
    wait_all(operands_in)

    def partial_sum(pr, at):
        a = transit[pr, at, 0].reshape(SIDE * depth, rank)
        b = transit[pr, at, 1].reshape(SIDE * depth, rank)
        return lax.dot_general(a, b, (((0,), (0,)), ((), ())), preferred_element_type=F32)

    partials_in = []
    for pr in (0, 1):
        at = place[1 - pr]
        for d in (1, -1, 2):
            there = wrap(at + d)
            partial[pr, there] = partial_sum(pr, there).astype(BF16)
            partials_in.append(send(partial.at[pr, there], arrived.at[pr, at], step[1 - pr](d)))

    rest_z = along_z(1, half // 2, count=half // 2)
    rest_x = along_x(1, half + half // 2, count=half // 2)
    first_z[1] = [some_z[0], rest_z[1]]
    first_x[1] = [some_x[0], rest_x[1]]
    totals = [partial_sum(pr, place[1 - pr]) for pr in (0, 1)]
    wait_all(partials_in)
    for pr in (0, 1):
        total = totals[pr]
        for d in (1, 2, 3):
            total = total + arrived[pr, wrap(place[1 - pr] + d)].astype(F32)
        cores[z, x, pr] = total.astype(BF16)
    core_in = []
    for pr in (0, 1):
        block = cores.at[z, x, pr]
        core_in.append([send(block, block, step[pr](d)) for d in (1, -1, 2)])

    first_z[-1] = along_z(-1, 0)
    first_x[-1] = along_x(-1, half)
    left_far = far_row(lefts, left_in)

    def line(pr, d, first, count):
        some = pl.ds(first, count)
        if pr == 0:
            return cores.at[wrap(z + d), some, 0]
        return cores.at[some, wrap(x + d), 1]

    line_in, line_far = [], []
    for pr in (0, 1):
        wait_all(core_in[pr])
        block = line(pr, 0, 0, SIDE)
        line_in.append([send(block, block, step[1 - pr](d)) for d in (1, -1)])

    wait_all(far_x[0] + far_z[0])
    first_z[2] = along_z(2, 0)
    first_x[2] = along_x(2, half)
    left_last = last_row(lefts, left_far)
    for pr in (0, 1):
        for k, d in ((0, 1), (1, -1)):
            line_in[pr][k].wait_recv()
            block = line(pr, -d, k * SIDE // 2, SIDE // 2)
            line_far.append(send(block, block, step[1 - pr](d)))

    for d in (-1, 1, 2):
        late_z[d] = along_z_far(d, 0, first_z[d])
        late_x[d] = along_x_far(d, half, first_x[d])

    wait_all([left_in[4], *left_far[2:], *left_last, *line_far])

    @pl.loop(0, n_pairs, unroll=4)
    def _(p):
        to = lax.div(p, 2)
        pr, tz, tx = lax.rem(p, 2), lax.div(to, SIDE), lax.rem(to, SIDE)
        product = jnp.dot(lefts[pairs[0, p]], cores[tz, tx, pr], preferred_element_type=F32)
        lead[p] = product.astype(BF16)

    width = SIDE * part
    get_here.wait()
    get_targets.wait()

    def update(dz):
        group = whole[dz]
        columns = pl.ds(pl.multiple_of(wrap(z + dz) * width, width), width)

        @pl.loop(0, n_pairs, unroll=32)
        def _(p):
            right = group[:, lax.rem(pairs[1, p], n_tiles)].reshape(width, rank)
            change = lax.dot_general(
                lead[p], right, (((1,), (1,)), ((), ())), preferred_element_type=F32
            )
            out[p, :, columns] = (out[p, :, columns].astype(F32) - change).astype(BF16)

    wait_all(late_x[0])
    update(0)
    wait_all([some_x[1], rest_x[0], some_z[1], rest_z[0]])
    wait_all(late_x[1] + late_x[-1])
    update(1)
    update(-1)
    wait_all(late_x[2] + [c for d in (0, -1, 1, 2) for c in late_z[d]])
    update(2)
    for copy in sent:
        copy.wait_send()


def shards(panel, bases, pivots, ranks, pairs, targets):
    n_tiles, depth, rank = panel.shape
    part = bases.shape[1]
    n_pairs = pairs.shape[0]
    n_rows = lax.axis_size("row")
    group = pltpu.VMEM((SIDE, n_tiles, part, rank), BF16)
    hbm = pl.BlockSpec(memory_space=pltpu.HBM)
    return pl.pallas_call(
        kernel,
        out_shape=jax.ShapeDtypeStruct(targets.shape, targets.dtype),
        in_specs=[hbm] * 6,
        out_specs=pl.BlockSpec(memory_space=pltpu.VMEM),
        scratch_shapes=[
            pltpu.SMEM(pivots.shape, F32),
            pltpu.SMEM(ranks.shape, jnp.int32),
            pltpu.SMEM((2, n_pairs), jnp.int32),
            group,
            group,
            group,
            group,
            pltpu.VMEM((n_rows * n_tiles, part, rank), BF16),
            pltpu.VMEM((n_rows * n_tiles, depth, rank), BF16),
            pltpu.VMEM((n_tiles, depth, rank), BF16),
            pltpu.VMEM((2, SIDE, SIDE, 2, depth, rank), BF16),
            pltpu.VMEM((2, SIDE, 2, SIDE, depth, rank), BF16),
            pltpu.VMEM((2, SIDE, rank, rank), BF16),
            pltpu.VMEM((2, SIDE, rank, rank), BF16),
            pltpu.VMEM((SIDE, SIDE, 2, rank, rank), BF16),
            pltpu.VMEM((n_pairs, part, rank), BF16),
            pltpu.VMEM((depth, rank), F32),
            pltpu.SemaphoreType.DMA((100,)),
            pltpu.SemaphoreType.DMA((100,)),
            pltpu.SemaphoreType.DMA((12,)),
        ],
        compiler_params=pltpu.CompilerParams(
            collective_id=0, has_side_effects=True, vmem_limit_bytes=48 << 20
        ),
    )(*(pltpu.with_memory_space_constraint(a, pltpu.HBM) for a in (panel, bases, pivots, ranks, pairs.T, targets)))


def solution(mesh):
    return jax.shard_map(
        shards,
        mesh=mesh,
        in_specs=(
            P("row", "col", None),
            P("row", "col", None),
            P("col"),
            P("row"),
            P("row", None),
            P("row", "col", None),
        ),
        out_specs=P("row", "col", None),
        check_vma=False,
    )
```
